1024 devices in a mesh: gx: 32 (over y, x), gy: 16 (over z), gz: 2 (over core).
Axes of the slice: x: 4, y: 8, z: 16, core: 2. Of those that a mesh axis runs over, the one named last changes fastest.
Arguments:
- s_blocks: bfloat16 [1024, 4, 128, 128], P(('gx', 'gy', 'gz')), may hold values from -1 to 2
- s_columns: int32 [1024, 4], P(('gx', 'gy', 'gz')), may hold values from 0 to 6, as said below
- new_home: int32 [1024], P(('gx', 'gy', 'gz')), may hold values from 0 to 1, as said below
- z_pattern: int32 [1024, 7], P(('gx', 'gy', 'gz')), may hold values 0 or 1
- y_pattern: int32 [1024, 7], P(('gx', 'gy', 'gz')), may hold values 0 or 1
Outputs:
- z_out: bfloat16 [1024, 128, 7, 128], P(('gx', 'gy', 'gz'))
- y_out: bfloat16 [1024, 128, 7, 128], P(('gx', 'gy', 'gz'))
The draws below stay inside these ranges and needn't reach their ends.
Inputs may be any that keep to these rules, and one draw needn't show every extreme that they name: new_home = 1 * (new gz index) + new slot; among the clusters of devices that share gx and gy indices each value occurs once, and the 1 clusters of one device go to 1 different devices. `s_columns`: the entries of a row are distinct, and the first is the cluster's own diagonal block in the new layout (part 0, its new slot).
All inputs are finite; a program needn't handle non-finite values. No bound on the sum of `z_pattern` or of `y_pattern` on one device may be relied on, other than what follows from the above.
Results may differ from the reference program's by a relative error of at most 0.0058.
Values may be sent and summed in bfloat16 or wider, within the bound.
A program may use at most 32 MiB of HBM per device.

```python
import math
import jax
import jax.numpy as jnp
from jax import lax

B = 128
SLOTS = 1
NB = 4
ITERS = 2
CLUSTERS = 1024
N_GX = 32
N_GY = 16
N_GZ = 2


def home_table(key):
    lines = N_GX * N_GY

    def one_line(line_key):
        first, second, third = jax.random.split(line_key, 3)
        shuffle = jax.random.permutation(first, N_GZ)
        offsets = jax.random.permutation(second, N_GZ)[:SLOTS]
        flips = jax.random.randint(third, (N_GZ,), 0, SLOTS)
        source = jnp.arange(N_GZ)[:, None]
        device = shuffle[(source + offsets[None, :]) % N_GZ]
        landing = (jnp.arange(SLOTS)[None, :] + flips[device]) % SLOTS
        return device * SLOTS + landing
    table = jax.vmap(one_line)(jax.random.split(key, lines))
    return table.reshape(-1).astype(jnp.int32)


def draw_new_home(key, part):
    return home_table(jax.random.fold_in(key, 7))


def draw_s_columns(key, part):
    homes = home_table(jax.random.fold_in(key, 7))
    landing = (homes % SLOTS).astype(jnp.int32)
    total = homes.shape[0]

    def one_row(row_key, own):
        picks = jax.random.permutation(row_key, 7 * SLOTS - 1)[:NB - 1].astype(jnp.int32)
        picks = picks + (picks >= own).astype(jnp.int32)
        return jnp.concatenate([own[None], picks])
    row_keys = jax.random.split(jax.random.fold_in(key, 19), total)
    return jax.vmap(one_row)(row_keys, landing).astype(jnp.int32)


def draw_s_blocks(key, part):
    spread = 0.45 / math.sqrt(NB * B)
    first = jax.random.fold_in(jax.random.fold_in(key, 31), 0)
    shape = (CLUSTERS, NB, B, B)
    noise = jax.random.normal(first, shape, jnp.float32)
    values = noise * spread
    values = values.at[:, 0].add(jnp.eye(B, dtype=jnp.float32))
    return values.astype(jnp.bfloat16)


def place_ends(entries, key, low, top_value):
    place = [jax.random.randint(jax.random.fold_in(key, axis), (), 0, length) for axis, length in enumerate(entries.shape)]
    main_axis = entries.shape.index(max(entries.shape))
    neighbour = place[:main_axis] + [(place[main_axis] + 1) % entries.shape[main_axis]] + place[main_axis + 1:]
    return entries.at[tuple(place)].set(low).at[tuple(neighbour)].set(top_value)


def setup_inputs(seed: int = 0) -> dict:
    key_list = jax.random.split(jax.random.key(seed), 6)
    return {
        "s_blocks": draw_s_blocks(jax.random.fold_in(key_list[5], 71), 0),
        "s_columns": draw_s_columns(jax.random.fold_in(key_list[5], 71), 0),
        "new_home": draw_new_home(jax.random.fold_in(key_list[5], 71), 0),
        "z_pattern": place_ends((jax.random.randint(key_list[3], (CLUSTERS, 7 * SLOTS), 0, 3) < 2).astype(jnp.int32), jax.random.fold_in(key_list[3], 1), 0, 1),
        "y_pattern": place_ends((jax.random.randint(key_list[4], (CLUSTERS, 7 * SLOTS), 0, 3) < 2).astype(jnp.int32), jax.random.fold_in(key_list[4], 1), 0, 1),
    }


SHIFTS = ((0, 1, 2), (0, -1, 1), (1, 1, 4), (1, -1, 3), (2, 1, 6), (2, -1, 5))


def neighbour_grid(matrix, axis_pos, offset):
    length = matrix.shape[axis_pos]
    zeros = jnp.zeros_like(lax.slice_in_dim(matrix, 0, 1, axis=axis_pos))
    if offset == 1:
        return jnp.concatenate([zeros, lax.slice_in_dim(matrix, 0, length - 1, axis=axis_pos)], axis=axis_pos)
    return jnp.concatenate([lax.slice_in_dim(matrix, 1, length, axis=axis_pos), zeros], axis=axis_pos)


def halo_grid(matrix):
    pieces = []
    for axis_pos, offset, facing in SHIFTS:
        nearby = neighbour_grid(matrix, axis_pos, offset)
        pieces.append(jnp.stack([nearby[..., :, 0, :], nearby[..., :, facing, :]], axis=-2))
    return jnp.stack(pieces, axis=3)


def block_product(left, right, halo):
    block_size = left.shape[0]
    left_wide = left.astype(jnp.float32)
    right_wide = right.astype(jnp.float32)
    halo_wide = halo.astype(jnp.float32)
    stacked = jnp.concatenate([right_wide[:, 0, :][None], halo_wide[:, :, 1, :]], axis=0).reshape(7 * block_size, block_size)
    own_column = jnp.dot(left_wide.reshape(block_size, 7 * block_size), stacked, precision=lax.Precision.HIGHEST)
    across = jnp.dot(left_wide[:, 0, :], right_wide[:, 1:, :].reshape(block_size, 6 * block_size), precision=lax.Precision.HIGHEST).reshape(block_size, 6, block_size)
    across = across + jnp.einsum("irj,rjk->irk", left_wide[:, 1:, :], halo_wide[:, :, 0, :], precision=lax.Precision.HIGHEST)
    return jnp.concatenate([own_column[:, None, :], across], axis=1)


def grid_product(left, right):
    halo = halo_grid(right)
    result = lax.map(lambda items: block_product(items[0], items[1], items[2]),
                     (left.reshape((-1,) + left.shape[3:]), right.reshape((-1,) + right.shape[3:]), halo.reshape((-1,) + halo.shape[3:])))
    return result.reshape(left.shape[:3] + result.shape[1:])


def masked(retain, matrix):
    shape = matrix.shape
    blocked = matrix.reshape(shape[:3] + (SLOTS, B, 7, SLOTS, B))
    chosen = jnp.where(retain[:, :, :, :, None, :, :, None], blocked, jnp.zeros((), matrix.dtype))
    return chosen.reshape(shape)


def reference(s_blocks, s_columns, new_home, z_pattern, y_pattern):
    lines = N_GX * N_GY
    per_line = N_GZ * SLOTS
    blocks = s_blocks.reshape(lines, per_line, NB, B, B)
    columns = s_columns.reshape(lines, per_line, NB)
    homes = new_home.reshape(lines, per_line).astype(jnp.int32)
    line_ids = jnp.arange(lines, dtype=jnp.int32)[:, None]
    placed = jnp.zeros_like(blocks).at[line_ids, homes].set(blocks)
    placed_cols = jnp.zeros_like(columns).at[line_ids, homes].set(columns)
    slot_ids = jnp.arange(7 * SLOTS, dtype=jnp.int32)
    dense = jnp.zeros((lines, per_line, B, 7 * SLOTS, B), jnp.bfloat16)
    for position in range(NB):
        hits = placed_cols[:, :, position][..., None] == slot_ids
        dense = dense + jnp.where(hits[:, :, None, :, None], placed[:, :, position][:, :, :, None, :], jnp.zeros((), jnp.bfloat16))
    rows_total = SLOTS * B
    start = dense.reshape(N_GX, N_GY, N_GZ, rows_total, 7, rows_total)
    place_x = jnp.arange(N_GX)[:, None, None] + jnp.zeros((N_GX, N_GY, N_GZ), jnp.int32)
    place_y = jnp.arange(N_GY)[None, :, None] + jnp.zeros((N_GX, N_GY, N_GZ), jnp.int32)
    place_z = jnp.arange(N_GZ)[None, None, :] + jnp.zeros((N_GX, N_GY, N_GZ), jnp.int32)
    valid = jnp.stack([place_x >= 0, place_x > 0, place_x < N_GX - 1, place_y > 0, place_y < N_GY - 1,
                       place_z > 0, place_z < N_GZ - 1], axis=-1)
    own_slot = jnp.arange(SLOTS)
    diagonal = (jnp.arange(7)[None, :, None] == 0) & (own_slot[:, None, None] == own_slot[None, None, :])
    shape_keep = (N_GX, N_GY, N_GZ, SLOTS, 7, SLOTS)
    retain_valid = jnp.broadcast_to(valid[:, :, :, None, :, None], shape_keep)
    retain_y = ((y_pattern.reshape(shape_keep) == 1) | diagonal) & valid[:, :, :, None, :, None]
    retain_z = ((z_pattern.reshape(shape_keep) == 1) | diagonal) & valid[:, :, :, None, :, None]
    identity = jnp.concatenate([jnp.eye(rows_total, dtype=jnp.float32)[:, None, :],
                                jnp.zeros((rows_total, 6, rows_total), jnp.float32)], axis=1)
    square = masked(retain_valid, start)
    inverse = jnp.broadcast_to(identity.astype(jnp.bfloat16), start.shape)
    for turn_index in range(ITERS):
        quad = masked(retain_y, grid_product(inverse, square))
        middle = masked(retain_y, 1.5 * identity - 0.5 * quad).astype(jnp.bfloat16)
        square_next = masked(retain_y, grid_product(square, middle)).astype(jnp.bfloat16)
        inverse = masked(retain_z, grid_product(middle, inverse)).astype(jnp.bfloat16)
        square = square_next
    out_shape = (CLUSTERS, B, 7 * SLOTS, B)
    return inverse.reshape(out_shape), square.reshape(out_shape)
```

```python
import jax
import jax.numpy as jnp
from jax import lax
from jax.experimental import pallas as pl
from jax.experimental.pallas import tpu as pltpu
from jax.sharding import PartitionSpec as P

MESH = pl.DeviceIdType.MESH
BLOCK = 128
SIDES = (1, 2, 3, 4, 5)
FACING = {1: 2, 2: 1, 3: 4, 4: 3, 5: 5}
FACE, OWN, NEXT, MIDDLE = range(4)


def dot(a, b):
    return jnp.dot(a, b, preferred_element_type=jnp.float32)


def kernel(
    sizes, s_hbm, columns_hbm, home_hbm, z_hbm, y_hbm, z_out, y_out,
    raw, columns, home, z_keep, y_keep, face_out, own_out, next_out, middle_out,
    face_in, own_in, next_in, middle_in, local_sem, move_send, move_recv, send, recv,
):
    n_x, n_y = sizes
    gx, gy, gz = lax.axis_index("gx"), lax.axis_index("gy"), lax.axis_index("gz")
    place = {1: (gx - 1, gy, gz), 2: (gx + 1, gy, gz), 3: (gx, gy - 1, gz), 4: (gx, gy + 1, gz), 5: (gx, gy, 1 - gz)}
    inside = {1: gx > 0, 2: gx < n_x - 1, 3: gy > 0, 4: gy < n_y - 1}
    slot = {1: 1, 2: 2, 3: 3, 4: 4, 5: 6 - gz}

    loads = [
        pltpu.make_async_copy(source, target, local_sem.at[i])
        for i, (source, target) in enumerate((
            (s_hbm, raw.at[0]), (columns_hbm, columns.at[0]), (home_hbm, home),
            (z_hbm, z_keep.at[0]), (y_hbm, y_keep),
        ))
    ]
    for load in loads:
        load.start()

    def on_side(c, run):
        if c in inside:
            pl.when(inside[c])(run)
        else:
            run()

    barrier = pltpu.get_barrier_semaphore()
    for c in SIDES:
        on_side(c, lambda c=c: pl.semaphore_signal(barrier, inc=1, device_id=place[c], device_id_type=MESH))
    count = 1 + sum(jnp.where(inside[c], 1, 0) for c in inside)
    pl.semaphore_wait(barrier, count)

    def remote(source, target, s_sem, r_sem, c):
        return pltpu.make_async_remote_copy(
            src_ref=source, dst_ref=target, send_sem=s_sem, recv_sem=r_sem, device_id=place[c], device_id_type=MESH
        )

    moves = [
        remote(columns_hbm, columns.at[1], move_send.at[0], move_recv.at[0], 5),
        remote(s_hbm, raw.at[1], move_send.at[1], move_recv.at[1], 5),
    ]
    for move in moves:
        move.start()
    keeps = {c: remote(z_hbm, z_keep.at[FACING[c]], send.at[4, c], recv.at[4, FACING[c]], c) for c in SIDES}
    def arrival(buffer, message, c):
        return pltpu.make_async_remote_copy(
            src_ref=buffer.at[c], dst_ref=buffer.at[c], send_sem=send.at[message, c], recv_sem=recv.at[message, c],
            device_id=place[c], device_id_type=MESH,
        )

    for c in SIDES:
        on_side(c, keeps[c].start)

    for load in loads[1:]:
        load.wait()
    loads[0].wait()
    for move in moves:
        move.wait()

    stay = home[0] == gz
    block = [jnp.where(stay, raw[0, k], raw[1, k]) for k in range(4)]
    column = [jnp.where(stay, columns[0, 0, k], columns[1, 0, k]) for k in range(4)]
    zero = jnp.zeros((BLOCK, BLOCK), jnp.bfloat16)
    square, keep_y, keep_z = {0: block[0]}, {}, {}
    for c in SIDES:
        valid = inside.get(c, True)
        found = zero
        for k in (1, 2, 3):
            found = jnp.where(jnp.logical_and(column[k] == slot[c], valid), block[k], found)
        square[c] = found
        keep_y[c] = jnp.logical_and(y_keep[0, slot[c]] == 1, valid)
        keep_z[c] = jnp.logical_and(z_keep[0, 0, slot[c]] == 1, valid)

    own_out[...] = square[0]
    face = {}
    for c in SIDES:
        face[c] = jnp.where(keep_y[c], square[c], zero)
        face_out[c] = face[c]
        if c in inside:
            @pl.when(jnp.logical_not(inside[c]))
            def _():
                for buffer in (face_in, own_in, next_in, middle_in):
                    buffer[c] = zero

    def send_to(source, target, message, c):
        return remote(source, target.at[FACING[c]], send.at[message, c], recv.at[message, FACING[c]], c)

    faces = {c: send_to(face_out.at[c], face_in, FACE, c) for c in SIDES}
    owns = {c: send_to(own_out, own_in, OWN, c) for c in SIDES}
    for c in SIDES:
        on_side(c, faces[c].start)
    for c in SIDES:
        on_side(c, owns[c].start)

    row = lax.broadcasted_iota(jnp.int32, (BLOCK, BLOCK), 0)
    lane = lax.broadcasted_iota(jnp.int32, (BLOCK, BLOCK), 1)
    lifted = jnp.where(row == lane, 1.5, 0.0).astype(jnp.float32)

    def half(x):
        return (x.astype(jnp.float32) * -0.5).astype(jnp.bfloat16)

    def centre(x):
        return (lifted - 0.5 * x.astype(jnp.float32)).astype(jnp.bfloat16)

    def kept(mask, x):
        return jnp.where(mask, x, jnp.zeros_like(x))

    middle = {0: centre(square[0])}
    inverse = {0: middle[0]}
    for c in SIDES:
        middle[c] = half(face[c])
        inverse[c] = kept(keep_z[c], middle[c])
    first = {c: dot(square[0], middle[c]) for c in (0,) + SIDES}

    for c in SIDES:
        on_side(c, arrival(face_in, FACE, c).wait_recv)
        on_side(c, arrival(z_keep, 4, c).wait_recv)
    near_face = {c: face_in[c] for c in SIDES}
    total = first[0]
    for c in SIDES:
        total = total - 0.5 * dot(square[c], near_face[c])
    square_next = {0: total.astype(jnp.bfloat16)}
    next_out[...] = square_next[0]
    nexts = {c: send_to(next_out, next_in, NEXT, c) for c in SIDES}
    for c in SIDES:
        on_side(c, nexts[c].start)

    near_middle = {c: half(near_face[c]) for c in SIDES}
    facing_slot = {1: 2, 2: 1, 3: 4, 4: 3, 5: 5 + gz}
    near_inverse = {}
    for c in SIDES:
        flag = jnp.logical_and(z_keep[c, 0, facing_slot[c]] == 1, inside.get(c, True))
        near_inverse[c] = kept(flag, near_middle[c])
    part_near_next = {c: dot(near_face[c], middle[0]) for c in SIDES}
    part_near_quad = {c: dot(near_inverse[c], square_next[0]) for c in SIDES}

    for c in SIDES:
        on_side(c, arrival(own_in, OWN, c).wait_recv)
    near_own = {c: own_in[c] for c in SIDES}
    near_centre = {c: centre(near_own[c]) for c in SIDES}
    near_next = {}
    for c in SIDES:
        near_next[c] = (part_near_next[c] + dot(near_own[c], near_middle[c])).astype(jnp.bfloat16)
    quad = dot(inverse[0], square_next[0])
    for c in SIDES:
        quad = quad + dot(inverse[c], near_next[c])
    last = {0: (lifted - 0.5 * quad).astype(jnp.bfloat16)}
    middle_out[...] = last[0]
    middles = {c: send_to(middle_out, middle_in, MIDDLE, c) for c in SIDES}
    for c in SIDES:
        on_side(c, middles[c].start)

    for c in SIDES:
        square_next[c] = kept(keep_y[c], first[c] + dot(square[c], near_centre[c])).astype(jnp.bfloat16)
    part_quad = {c: dot(inverse[0], square_next[c]) for c in SIDES}
    y_total = dot(square_next[0], last[0])
    for c in SIDES:
        near_last = (-0.5 * (part_near_quad[c] + dot(near_centre[c], near_next[c]))).astype(jnp.bfloat16)
        y_total = y_total + dot(square_next[c], near_last)
    y_out[0] = y_total.astype(jnp.bfloat16)

    z_total = dot(last[0], inverse[0])
    z_part = {c: dot(last[0], inverse[c]) for c in SIDES}
    for c in SIDES:
        on_side(c, arrival(next_in, NEXT, c).wait_recv)
    for c in SIDES:
        whole = part_quad[c] + dot(inverse[c], next_in[c])
        last[c] = kept(keep_y[c], -0.5 * whole).astype(jnp.bfloat16)
        z_total = z_total + dot(last[c], near_inverse[c])
        z_part[c] = z_part[c] + dot(last[c], near_centre[c])
    z_out[0] = z_total.astype(jnp.bfloat16)
    for c in SIDES:
        z_out[slot[c]] = kept(keep_z[c], z_part[c]).astype(jnp.bfloat16)
    z_out[facing_slot[5]] = zero
    y_out[facing_slot[5]] = zero
    y_part = {c: dot(square_next[0], last[c]) for c in SIDES}
    for c in SIDES:
        on_side(c, arrival(middle_in, MIDDLE, c).wait_recv)
    for c in SIDES:
        y_out[slot[c]] = kept(keep_y[c], y_part[c] + dot(square_next[c], middle_in[c])).astype(jnp.bfloat16)
    for group in (keeps, faces, owns, nexts, middles):
        for c in SIDES:
            on_side(c, group[c].wait_send)


def solution(mesh):
    sizes = (mesh.shape["gx"], mesh.shape["gy"])

    def step(s_blocks, s_columns, new_home, z_pattern, y_pattern):
        any_spec = pl.BlockSpec(memory_space=pl.ANY)
        vmem = pl.BlockSpec(memory_space=pltpu.VMEM)
        blocks = jax.ShapeDtypeStruct((7, BLOCK, BLOCK), jnp.bfloat16)
        buffer = pltpu.VMEM((6, BLOCK, BLOCK), jnp.bfloat16)
        single = pltpu.VMEM((BLOCK, BLOCK), jnp.bfloat16)
        dma = pltpu.SemaphoreType.DMA
        z, y = pl.pallas_call(
            lambda *refs: kernel(sizes, *refs),
            name="newton_schulz",
            out_shape=(blocks, blocks),
            in_specs=[any_spec] * 5,
            out_specs=(vmem, vmem),
            scratch_shapes=[
                pltpu.VMEM((2, 4, BLOCK, BLOCK), jnp.bfloat16),
                pltpu.SMEM((2, 1, 4), jnp.int32),
                pltpu.SMEM((1,), jnp.int32),
                pltpu.SMEM((6, 1, 7), jnp.int32),
                pltpu.SMEM((1, 7), jnp.int32),
                buffer, single, single, single,
                buffer, buffer, buffer, buffer,
                dma((5,)), dma((2,)), dma((2,)), dma((5, 6)), dma((5, 6)),
            ],
            compiler_params=pltpu.CompilerParams(collective_id=0, has_side_effects=True),
        )(s_blocks[0], s_columns, new_home, z_pattern, y_pattern)
        return jnp.transpose(z, (1, 0, 2))[None], jnp.transpose(y, (1, 0, 2))[None]

    row = P(("gx", "gy", "gz"))
    wide = P(("gx", "gy", "gz"), None)
    block = P(("gx", "gy", "gz"), None, None, None)
    return jax.shard_map(
        step, mesh=mesh, in_specs=(block, wide, row, wide, wide), out_specs=(block, block), check_vma=False
    )
```

```python
import jax
import jax.numpy as jnp
from jax import lax
from jax.experimental import pallas as pl
from jax.experimental.pallas import tpu as pltpu
from jax.sharding import PartitionSpec as P

MESH = pl.DeviceIdType.MESH
BLOCK = 128
LINKS = (1, 2, 3, 4)
SIDES = LINKS + (5,)
FACING = {1: 2, 2: 1, 3: 4, 4: 3, 5: 5}


def dot(a, b):
    return jnp.dot(a, b, preferred_element_type=jnp.float32)


def beside(parts):
    return jnp.concatenate(parts, axis=1)


def below(parts):
    return jnp.concatenate(parts, axis=0)


def kernel(
    sizes, s_hbm, columns_hbm, home_hbm, z_hbm, y_hbm, z_out, y_out,
    raw, columns, home, z_keep, y_keep, face_out, own_out, next_out, middle_out,
    face_in, own_in, next_in, middle_in, local_sem, pair_sem, move, row_send, row_recv,
    send, face_recv, own_recv, next_recv, middle_recv,
):
    n_x, n_y = sizes
    gx, gy, gz = lax.axis_index("gx"), lax.axis_index("gy"), lax.axis_index("gz")
    place = {1: (gx - 1, gy, gz), 2: (gx + 1, gy, gz), 3: (gx, gy - 1, gz), 4: (gx, gy + 1, gz), 5: (gx, gy, 1 - gz)}
    inside = {1: gx > 0, 2: gx < n_x - 1, 3: gy > 0, 4: gy < n_y - 1}
    slot = {1: 1, 2: 2, 3: 3, 4: 4, 5: 6 - gz}
    facing_slot = {1: 2, 2: 1, 3: 4, 4: 3, 5: 5 + gz}

    loads = [
        pltpu.make_async_copy(source, target, local_sem.at[i])
        for i, (source, target) in enumerate((
            (s_hbm, raw.at[pl.ds(0, 4)]), (columns_hbm, columns.at[0]), (home_hbm, home),
            (z_hbm, z_keep.at[0]), (y_hbm, y_keep),
        ))
    ]

    def on_side(c, run):
        if c in inside:
            pl.when(inside[c])(run)
        else:
            run()

    for load in loads:
        load.start()
    low, high = gz == 0, gz == 1
    barrier = pltpu.get_barrier_semaphore()

    def signal(semaphore, device):
        pl.semaphore_signal(semaphore, inc=1, device_id=device, device_id_type=MESH)

    @pl.when(high)
    def _():
        signal(barrier, place[5])

    @pl.when(low)
    def _():
        pl.semaphore_wait(barrier, 1)
        signal(pair_sem, place[5])

    @pl.when(high)
    def _():
        pl.semaphore_wait(pair_sem, 1)
        for c in LINKS:
            @pl.when(inside[c])
            def _():
                signal(barrier, place[c])

    def remote(source, target, s_sem, r_sem, device):
        return pltpu.make_async_remote_copy(
            src_ref=source, dst_ref=target, send_sem=s_sem, recv_sem=r_sem, device_id=device, device_id_type=MESH
        )

    moves = [
        remote(columns_hbm, columns.at[1], move.at[0], move.at[1], place[5]),
        remote(s_hbm, raw.at[pl.ds(4, 4)], move.at[2], move.at[3], place[5]),
    ]
    moves[0].start()

    @pl.when(low)
    def _():
        moves[1].start()

    loads[0].wait()

    @pl.when(high)
    def _():
        remote(raw.at[pl.ds(0, 4)], raw.at[pl.ds(4, 4)], move.at[2], move.at[3], place[5]).start()
        pl.semaphore_wait(barrier, sum(jnp.where(inside[c], 1, 0) for c in LINKS))
        signal(pair_sem, place[5])

    @pl.when(low)
    def _():
        pl.semaphore_wait(pair_sem, 1)

    def row_copy(c, end):
        return remote(z_hbm, z_keep.at[end], row_send.at[c], row_recv.at[end], place[c])

    for c in SIDES:
        on_side(c, row_copy(c, FACING[c]).start)

    def send_to(source, target, sems):
        for c in SIDES:
            part = source.at[c] if len(source.shape) == 3 else source
            on_side(c, remote(part, target.at[FACING[c]], send.at[c], sems.at[FACING[c]], place[c]).start)

    def arrived(buffer, sems, c):
        on_side(c, remote(buffer.at[c], buffer.at[c], send.at[c], sems.at[c], place[c]).wait_recv)

    zero = jnp.zeros((BLOCK, BLOCK), jnp.bfloat16)
    raw[8] = zero
    for c in LINKS:
        @pl.when(jnp.logical_not(inside[c]))
        def _():
            for buffer in (face_in, own_in, next_in, middle_in):
                buffer[c] = zero
            for i in range(7):
                z_keep[c, 0, i] = 0
    for load in loads[1:]:
        load.wait()
    moves[0].wait_recv()
    stay = home[0, 0] == gz
    base = jnp.where(stay, 0, 4)
    column = [jnp.where(stay, columns[0, 0, k], columns[1, 0, k]) for k in range(4)]
    found, kept_found, keep_y, keep_z = {}, {}, {}, {}
    for c in SIDES:
        valid = inside.get(c, True)
        index = jnp.int32(8)
        for k in (1, 2, 3):
            index = jnp.where(column[k] == slot[c], base + k, index)
        keep_y[c] = jnp.logical_and(y_keep[0, slot[c]] == 1, valid)
        keep_z[c] = jnp.logical_and(z_keep[0, 0, slot[c]] == 1, valid)
        found[c] = jnp.where(valid, index, 8)
        kept_found[c] = jnp.where(keep_y[c], index, 8)
    moves[1].wait_recv()

    face = {}
    for c in SIDES:
        face[c] = raw[kept_found[c]]
        face_out[c] = face[c]
    square = {0: raw[base]}
    own_out[...] = square[0]
    send_to(face_out, face_in, face_recv)
    for c in LINKS:
        on_side(c, remote(own_out, own_in.at[FACING[c]], send.at[c], own_recv.at[FACING[c]], place[c]).start)

    row = lax.broadcasted_iota(jnp.int32, (BLOCK, BLOCK), 0)
    lane = lax.broadcasted_iota(jnp.int32, (BLOCK, BLOCK), 1)
    lifted = jnp.where(row == lane, 1.5, 0.0).astype(jnp.float32)

    def half(x):
        return (x.astype(jnp.float32) * -0.5).astype(jnp.bfloat16)

    def centre(x):
        return (lifted - 0.5 * x.astype(jnp.float32)).astype(jnp.bfloat16)

    def kept(mask, x):
        return jnp.where(mask, x, jnp.zeros_like(x))

    moves[0].wait_send()

    middle = {0: centre(square[0])}
    inverse = {0: middle[0]}
    for c in SIDES:
        square[c] = raw[found[c]]
        middle[c] = half(face[c])
        inverse[c] = kept(keep_z[c], middle[c])
    first = {c: dot(square[0], middle[c]) for c in (0,) + SIDES}
    near_flag = {}
    for c in SIDES:
        on_side(c, row_copy(c, c).wait_recv)
        near_flag[c] = jnp.logical_and(z_keep[c, 0, facing_slot[c]] == 1, inside.get(c, True))

    for c in SIDES:
        arrived(face_in, face_recv, c)
    near_face = {c: face_in[c] for c in SIDES}
    total = first[0] - 0.5 * dot(beside([square[c] for c in SIDES]), below([near_face[c] for c in SIDES]))
    square_next = {0: total.astype(jnp.bfloat16)}
    next_out[...] = square_next[0]
    send_to(next_out, next_in, next_recv)

    spread = dot(below([near_face[c] for c in SIDES]), middle[0])
    for c in LINKS:
        arrived(own_in, own_recv, c)
    near_own, near_next = {}, {}
    for i, c in enumerate(SIDES):
        near_own[c] = raw[4 - base] if c == 5 else own_in[c]
        part = spread[i * BLOCK:(i + 1) * BLOCK]
        near_next[c] = (part - 0.5 * dot(near_own[c], near_face[c])).astype(jnp.bfloat16)
    quad = dot(
        beside([inverse[c] for c in (0,) + SIDES]), below([square_next[0]] + [near_next[c] for c in SIDES])
    )
    last = {0: (lifted - 0.5 * quad).astype(jnp.bfloat16)}
    middle_out[...] = last[0]
    send_to(middle_out, middle_in, middle_recv)
    moves[1].wait_send()

    near_centre, near_inverse, near_last, part_quad = {}, {}, {}, {}
    for c in SIDES:
        near_centre[c] = centre(near_own[c])
        square_next[c] = kept(keep_y[c], first[c] + dot(square[c], near_centre[c])).astype(jnp.bfloat16)
        near_inverse[c] = kept(near_flag[c], half(near_face[c]))
        part_quad[c] = dot(inverse[0], square_next[c])
        near_quad = dot(beside([near_inverse[c], near_centre[c]]), below([square_next[0], near_next[c]]))
        near_last[c] = (-0.5 * near_quad).astype(jnp.bfloat16)
    y_total = dot(
        beside([square_next[c] for c in (0,) + SIDES]), below([last[0]] + [near_last[c] for c in SIDES])
    )
    y_out[0] = y_total.astype(jnp.bfloat16)
    z_out[facing_slot[5]] = zero
    y_out[facing_slot[5]] = zero

    for c in SIDES:
        arrived(next_in, next_recv, c)
    y_part = {}
    for c in SIDES:
        last[c] = kept(keep_y[c], -0.5 * (part_quad[c] + dot(inverse[c], next_in[c]))).astype(jnp.bfloat16)
        z_part = dot(beside([last[0], last[c]]), below([inverse[c], near_centre[c]]))
        z_out[slot[c]] = kept(keep_z[c], z_part).astype(jnp.bfloat16)
        y_part[c] = dot(square_next[0], last[c])
    z_total = dot(
        beside([last[c] for c in (0,) + SIDES]), below([inverse[0]] + [near_inverse[c] for c in SIDES])
    )
    z_out[0] = z_total.astype(jnp.bfloat16)

    for c in SIDES:
        arrived(middle_in, middle_recv, c)
    for c in SIDES:
        y_out[slot[c]] = kept(keep_y[c], y_part[c] + dot(square_next[c], middle_in[c])).astype(jnp.bfloat16)

    def drained(c, blocks):
        part = raw.at[pl.ds(0, blocks)]
        remote(part, part, send.at[c], face_recv.at[c], place[c]).wait_send()
        row_copy(c, c).wait_send()

    drained(5, 3)
    for c in LINKS:
        @pl.when(inside[c])
        def _():
            drained(c, 4)


def store(z_in, y_in, z_out, y_out, sem):
    copies = [pltpu.make_async_copy(z_in, z_out, sem.at[0]), pltpu.make_async_copy(y_in, y_out, sem.at[1])]
    for copy in copies:
        copy.start()
    for copy in copies:
        copy.wait()


def solution(mesh):
    sizes = (mesh.shape["gx"], mesh.shape["gy"])

    def step(s_blocks, s_columns, new_home, z_pattern, y_pattern):
        any_spec = pl.BlockSpec(memory_space=pl.ANY)
        vmem = pl.BlockSpec(memory_space=pltpu.VMEM)
        buffer = pltpu.VMEM((6, BLOCK, BLOCK), jnp.bfloat16)
        single = pltpu.VMEM((BLOCK, BLOCK), jnp.bfloat16)
        dma = pltpu.SemaphoreType.DMA
        z, y = pl.pallas_call(
            lambda *refs: kernel(sizes, *refs),
            name="newton_schulz",
            out_shape=(pltpu.VMEM((7, BLOCK, BLOCK), jnp.bfloat16),) * 2,
            in_specs=[any_spec] * 5,
            out_specs=(vmem, vmem),
            scratch_shapes=[
                pltpu.VMEM((9, BLOCK, BLOCK), jnp.bfloat16),
                pltpu.SMEM((2, 1, 4), jnp.int32),
                pltpu.SMEM((1, 1), jnp.int32),
                pltpu.SMEM((6, 1, 7), jnp.int32),
                pltpu.SMEM((1, 7), jnp.int32),
                buffer, single, single, single,
                buffer, buffer, buffer, buffer,
                dma((5,)), pltpu.SemaphoreType.REGULAR, dma((4,)), dma((6,)), dma((6,)),
                dma((6,)), dma((6,)), dma((6,)), dma((6,)), dma((6,)),
            ],
            compiler_params=pltpu.CompilerParams(collective_id=0, has_side_effects=True),
        )(s_blocks[0], s_columns, new_home.reshape(1, 1), z_pattern, y_pattern)
        z, y = pl.pallas_call(
            store,
            name="store",
            out_shape=(jax.ShapeDtypeStruct((7, BLOCK, BLOCK), jnp.bfloat16),) * 2,
            in_specs=[any_spec] * 2,
            out_specs=(any_spec,) * 2,
            scratch_shapes=[dma((2,))],
            compiler_params=pltpu.CompilerParams(vmem_limit_bytes=1 << 20),
        )(z, y)
        return jnp.transpose(z, (1, 0, 2))[None], jnp.transpose(y, (1, 0, 2))[None]

    row = P(("gx", "gy", "gz"))
    wide = P(("gx", "gy", "gz"), None)
    block = P(("gx", "gy", "gz"), None, None, None)
    return jax.shard_map(
        step, mesh=mesh, in_specs=(block, wide, row, wide, wide), out_specs=(block, block), check_vma=False
    )
```

```python
import functools

import jax
import jax.numpy as jnp
from jax import lax
from jax.experimental import pallas as pl
from jax.experimental.pallas import tpu as pltpu
from jax.sharding import PartitionSpec as P

MESH = pl.DeviceIdType.MESH
BLOCK = 128
LINKS = (1, 2, 3, 4)
SIDES = LINKS + (5,)
FACING = {1: 2, 2: 1, 3: 4, 4: 3, 5: 5}


def dot(a, b):
    return jnp.dot(a, b, preferred_element_type=jnp.float32)


def beside(parts):
    return jnp.concatenate(parts, axis=1)


def below(parts):
    return jnp.concatenate(parts, axis=0)


def at_once(lefts, rights):
    return dot(beside(lefts), below(rights))


def each(lefts, rights):
    return functools.reduce(jnp.add, [dot(left, right) for left, right in zip(lefts, rights)])


def kernel(
    sizes, s_hbm, columns_hbm, home_hbm, z_hbm, y_hbm, z_out, y_out,
    raw, columns, home, z_keep, y_keep, face_out, own_out, next_out, middle_out,
    face_in, own_in, next_in, middle_in, local_sem, pair_sem, move, z_send, z_recv, y_sem,
    send, face_recv, own_recv, next_recv, middle_recv,
):
    n_x, n_y = sizes
    gx, gy, gz = lax.axis_index("gx"), lax.axis_index("gy"), lax.axis_index("gz")
    place = {1: (gx - 1, gy, gz), 2: (gx + 1, gy, gz), 3: (gx, gy - 1, gz), 4: (gx, gy + 1, gz), 5: (gx, gy, 1 - gz)}
    inside = {1: gx > 0, 2: gx < n_x - 1, 3: gy > 0, 4: gy < n_y - 1}
    slot = {1: 1, 2: 2, 3: 3, 4: 4, 5: 6 - gz}
    facing_slot = {1: 2, 2: 1, 3: 4, 4: 3, 5: 5 + gz}
    low, high = gz == 0, gz == 1

    loads = [
        pltpu.make_async_copy(source, target, local_sem.at[i])
        for i, (source, target) in enumerate((
            (s_hbm, raw.at[pl.ds(0, 4)]), (columns_hbm, columns.at[0]), (home_hbm, home),
            (z_hbm, z_keep.at[0]), (y_hbm, y_keep.at[0]),
        ))
    ]

    def on_side(c, run):
        if c in inside:
            pl.when(inside[c])(run)
        else:
            run()

    def remote(source, target, s_sem, r_sem, device):
        return pltpu.make_async_remote_copy(
            src_ref=source, dst_ref=target, send_sem=s_sem, recv_sem=r_sem, device_id=device, device_id_type=MESH
        )

    for load in loads:
        load.start()
    barrier = pltpu.get_barrier_semaphore()

    def signal(semaphore, device):
        pl.semaphore_signal(semaphore, inc=1, device_id=device, device_id_type=MESH)

    @pl.when(high)
    def _():
        signal(barrier, place[5])

    moves = [
        remote(columns_hbm, columns.at[1], move.at[0], move.at[1], place[5]),
        remote(s_hbm, raw.at[pl.ds(4, 4)], move.at[2], move.at[3], place[5]),
    ]

    @pl.when(low)
    def _():
        pl.semaphore_wait(barrier, 1)
        signal(pair_sem, place[5])
        moves[1].start()
        moves[0].start()

    for c in LINKS:
        @pl.when(inside[c])
        def _():
            x, y, _ = place[c]
            signal(barrier, (x, y, 1))

    zero = jnp.zeros((BLOCK, BLOCK), jnp.bfloat16)
    raw[8] = zero

    loads[0].wait()

    @pl.when(high)
    def _():
        pl.semaphore_wait(pair_sem, 1)
        remote(raw.at[pl.ds(0, 4)], raw.at[pl.ds(4, 4)], move.at[2], move.at[3], place[5]).start()
        moves[0].start()
        pl.semaphore_wait(barrier, sum(jnp.where(inside[c], 2, 0) for c in LINKS))
        signal(pair_sem, place[5])

    for load in loads[1:]:
        load.wait()

    def z_copy(c, end):
        return remote(z_hbm, z_keep.at[end], z_send.at[c - 1], z_recv.at[end - 1], place[c])

    y_copy = remote(y_hbm, y_keep.at[1], y_sem.at[0], y_sem.at[1], place[5])
    y_copy.start()
    z_copy(5, 5).start()
    moves[0].wait_recv()
    stay = home[0, 0] == gz
    base = jnp.where(stay, 0, 4)
    column = [jnp.where(stay, columns[0, 0, k], columns[1, 0, k]) for k in range(4)]
    other_column = [jnp.where(stay, columns[1, 0, k], columns[0, 0, k]) for k in range(4)]

    def pick(entries, wanted, first):
        index = jnp.int32(8)
        for k in (1, 2, 3):
            index = jnp.where(entries[k] == wanted, first + k, index)
        return index

    found, kept_found, keep_y, keep_z = {}, {}, {}, {}
    for c in SIDES:
        valid = inside.get(c, True)
        index = pick(column, slot[c], base)
        keep_y[c] = jnp.logical_and(y_keep[0, 0, slot[c]] == 1, valid)
        keep_z[c] = jnp.logical_and(z_keep[0, 0, slot[c]] == 1, valid)
        found[c] = jnp.where(valid, index, 8)
        kept_found[c] = jnp.where(keep_y[c], index, 8)

    moves[1].wait_recv()
    square = {0: raw[base]}
    own_out[...] = square[0]
    for c in LINKS:
        face_out[c] = raw[kept_found[c]]

    @pl.when(low)
    def _():
        pl.semaphore_wait(pair_sem, 1)

    for c in LINKS:
        on_side(c, remote(face_out.at[c], face_in.at[FACING[c]], send.at[c - 1], face_recv.at[FACING[c] - 1], place[c]).start)
    for c in LINKS:
        on_side(c, remote(own_out, own_in.at[FACING[c]], send.at[c - 1], own_recv.at[FACING[c] - 1], place[c]).start)
    for c in LINKS:
        on_side(c, z_copy(c, FACING[c]).start)
    moves[0].wait_send()

    for c in LINKS:
        @pl.when(jnp.logical_not(inside[c]))
        def _():
            for buffer in (face_in, own_in, next_in, middle_in):
                buffer[c] = zero
            for i in range(7):
                z_keep[c, 0, i] = 0

    def send_to(source, target, sems):
        for c in SIDES:
            on_side(c, remote(source, target.at[FACING[c]], send.at[c - 1], sems.at[FACING[c] - 1], place[c]).start)

    def arrived(buffer, sems, c):
        on_side(c, remote(buffer.at[c], buffer.at[c], send.at[c - 1], sems.at[c - 1], place[c]).wait_recv)

    row = lax.broadcasted_iota(jnp.int32, (BLOCK, BLOCK), 0)
    lane = lax.broadcasted_iota(jnp.int32, (BLOCK, BLOCK), 1)
    lifted = jnp.where(row == lane, 1.5, 0.0).astype(jnp.float32)

    def half(x):
        return (x.astype(jnp.float32) * -0.5).astype(jnp.bfloat16)

    def centre(x):
        return (lifted - 0.5 * x.astype(jnp.float32)).astype(jnp.bfloat16)

    def kept(mask, x):
        return jnp.where(mask, x, jnp.zeros_like(x))


    middle = {0: centre(square[0])}
    inverse = {0: middle[0]}
    for c in SIDES:
        square[c] = raw[found[c]]
        middle[c] = half(raw[kept_found[c]])
        inverse[c] = kept(keep_z[c], middle[c])
    first = {c: dot(square[0], middle[c]) for c in (0,) + SIDES}
    moves[1].wait_send()
    y_copy.wait_recv()
    near_index = pick(other_column, facing_slot[5], 4 - base)

    for c in LINKS:
        arrived(face_in, face_recv, c)
    near_face = {c: face_in[c] for c in LINKS}
    near_face[5] = raw[jnp.where(y_keep[1, 0, facing_slot[5]] == 1, near_index, 8)]
    total = first[0] - 0.5 * at_once([square[c] for c in SIDES], [near_face[c] for c in SIDES])
    square_next = {0: total.astype(jnp.bfloat16)}
    next_out[...] = square_next[0]
    send_to(next_out, next_in, next_recv)

    spread = dot(below([near_face[c] for c in SIDES]), middle[0])
    near_own, near_next = {5: raw[4 - base]}, {}
    for c in LINKS:
        arrived(own_in, own_recv, c)
    for i, c in enumerate(SIDES):
        if c in LINKS:
            near_own[c] = own_in[c]
        part = spread[i * BLOCK:(i + 1) * BLOCK]
        near_next[c] = (part - 0.5 * dot(near_own[c], near_face[c])).astype(jnp.bfloat16)
    quad = each([inverse[c] for c in (0,) + SIDES], [square_next[0]] + [near_next[c] for c in SIDES])
    last = {0: (lifted - 0.5 * quad).astype(jnp.bfloat16)}
    middle_out[...] = last[0]
    send_to(middle_out, middle_in, middle_recv)
    y_copy.wait_send()

    near_flag = {}
    for c in SIDES:
        on_side(c, z_copy(c, c).wait_recv)
        near_flag[c] = jnp.logical_and(z_keep[c, 0, facing_slot[c]] == 1, inside.get(c, True))
    near_centre, near_inverse, near_last, part_quad, part_z = {}, {}, {}, {}, {0: dot(last[0], inverse[0])}
    for c in SIDES:
        near_centre[c] = centre(near_own[c])
        square_next[c] = kept(keep_y[c], first[c] + dot(square[c], near_centre[c])).astype(jnp.bfloat16)
        part_quad[c] = dot(inverse[0], square_next[c])
        part_z[c] = dot(last[0], inverse[c])
        near_inverse[c] = kept(near_flag[c], half(near_face[c]))
        near_quad = dot(beside([near_inverse[c], near_centre[c]]), below([square_next[0], near_next[c]]))
        near_last[c] = (-0.5 * near_quad).astype(jnp.bfloat16)
    y_total = at_once([square_next[c] for c in (0,) + SIDES], [last[0]] + [near_last[c] for c in SIDES])
    y_out[0] = y_total.astype(jnp.bfloat16)
    z_out[facing_slot[5]] = zero
    y_out[facing_slot[5]] = zero

    for c in SIDES:
        arrived(next_in, next_recv, c)
    for c in SIDES:
        last[c] = kept(keep_y[c], -0.5 * (part_quad[c] + dot(inverse[c], next_in[c]))).astype(jnp.bfloat16)
    z_total, y_part = part_z[0], {}
    for c in SIDES:
        wide = dot(last[c], beside([near_inverse[c], near_centre[c]]))
        z_total = z_total + wide[:, :BLOCK]
        z_out[slot[c]] = kept(keep_z[c], part_z[c] + wide[:, BLOCK:]).astype(jnp.bfloat16)
    y_wide = dot(square_next[0], beside([last[c] for c in SIDES]))
    y_part = {c: y_wide[:, i * BLOCK:(i + 1) * BLOCK] for i, c in enumerate(SIDES)}
    z_out[0] = z_total.astype(jnp.bfloat16)

    for c in SIDES:
        arrived(middle_in, middle_recv, c)
    for c in SIDES:
        y_out[slot[c]] = kept(keep_y[c], y_part[c] + dot(square_next[c], middle_in[c])).astype(jnp.bfloat16)

    for c in SIDES:
        @functools.partial(on_side, c)
        def _():
            part = raw.at[pl.ds(0, 2 if c == 5 else 4)]
            remote(part, part, send.at[c - 1], face_recv.at[0], place[c]).wait_send()
            z_copy(c, c).wait_send()


def store(z_in, y_in, z_out, y_out, sem):
    copies = [pltpu.make_async_copy(z_in, z_out, sem.at[0]), pltpu.make_async_copy(y_in, y_out, sem.at[1])]
    for copy in copies:
        copy.start()
    for copy in copies:
        copy.wait()


def solution(mesh):
    sizes = (mesh.shape["gx"], mesh.shape["gy"])

    def step(s_blocks, s_columns, new_home, z_pattern, y_pattern):
        any_spec = pl.BlockSpec(memory_space=pl.ANY)
        vmem = pl.BlockSpec(memory_space=pltpu.VMEM)
        buffer = pltpu.VMEM((6, BLOCK, BLOCK), jnp.bfloat16)
        single = pltpu.VMEM((BLOCK, BLOCK), jnp.bfloat16)
        dma = pltpu.SemaphoreType.DMA
        z, y = pl.pallas_call(
            lambda *refs: kernel(sizes, *refs),
            name="newton_schulz",
            out_shape=(pltpu.VMEM((7, BLOCK, BLOCK), jnp.bfloat16),) * 2,
            in_specs=[any_spec] * 5,
            out_specs=(vmem, vmem),
            scratch_shapes=[
                pltpu.VMEM((9, BLOCK, BLOCK), jnp.bfloat16),
                pltpu.SMEM((2, 1, 4), jnp.int32),
                pltpu.SMEM((1, 1), jnp.int32),
                pltpu.SMEM((6, 1, 7), jnp.int32),
                pltpu.SMEM((2, 1, 7), jnp.int32),
                buffer, single, single, single,
                buffer, buffer, buffer, buffer,
                dma((5,)), pltpu.SemaphoreType.REGULAR, dma((4,)), dma((5,)), dma((5,)), dma((2,)),
                dma((5,)), dma((4,)), dma((4,)), dma((5,)), dma((5,)),
            ],
            compiler_params=pltpu.CompilerParams(collective_id=0, has_side_effects=True),
        )(s_blocks[0], s_columns, new_home.reshape(1, 1), z_pattern, y_pattern)
        z, y = pl.pallas_call(
            store,
            name="store",
            out_shape=(jax.ShapeDtypeStruct((7, BLOCK, BLOCK), jnp.bfloat16),) * 2,
            in_specs=[any_spec] * 2,
            out_specs=(any_spec,) * 2,
            scratch_shapes=[dma((2,))],
            compiler_params=pltpu.CompilerParams(vmem_limit_bytes=1 << 20),
        )(z, y)
        return jnp.transpose(z, (1, 0, 2))[None], jnp.transpose(y, (1, 0, 2))[None]

    row = P(("gx", "gy", "gz"))
    wide = P(("gx", "gy", "gz"), None)
    block = P(("gx", "gy", "gz"), None, None, None)
    return jax.shard_map(
        step, mesh=mesh, in_specs=(block, wide, row, wide, wide), out_specs=(block, block), check_vma=False
    )
```

```python
import functools

import jax
import jax.numpy as jnp
from jax import lax
from jax.experimental import pallas as pl
from jax.experimental.pallas import tpu as pltpu
from jax.sharding import PartitionSpec as P

MESH = pl.DeviceIdType.MESH
BLOCK = 128
LINKS = (1, 2, 3, 4)
SIDES = LINKS + (5,)
FACING = {1: 2, 2: 1, 3: 4, 4: 3, 5: 5}


def dot(a, b):
    return jnp.dot(a, b, preferred_element_type=jnp.float32)


def beside(parts):
    return jnp.concatenate(parts, axis=1)


def below(parts):
    return jnp.concatenate(parts, axis=0)


def at_once(lefts, rights):
    return dot(beside(lefts), below(rights))


def each(lefts, rights):
    return functools.reduce(jnp.add, [dot(left, right) for left, right in zip(lefts, rights)])


def kernel(
    sizes, s_hbm, columns_hbm, home_hbm, z_hbm, y_hbm, z_out, y_out,
    raw, columns, home, z_keep, y_keep, face_out, own_out, next_out, middle_out,
    face_in, own_in, next_in, middle_in, local_sem, pair_sem, move, z_send, z_recv, y_sem,
    send, face_recv, own_recv, next_recv, middle_recv,
):
    n_x, n_y = sizes
    gx, gy, gz = lax.axis_index("gx"), lax.axis_index("gy"), lax.axis_index("gz")
    place = {1: (gx - 1, gy, gz), 2: (gx + 1, gy, gz), 3: (gx, gy - 1, gz), 4: (gx, gy + 1, gz), 5: (gx, gy, 1 - gz)}
    inside = {1: gx > 0, 2: gx < n_x - 1, 3: gy > 0, 4: gy < n_y - 1}
    slot = {1: 1, 2: 2, 3: 3, 4: 4, 5: 6 - gz}
    facing_slot = {1: 2, 2: 1, 3: 4, 4: 3, 5: 5 + gz}
    low, high = gz == 0, gz == 1

    loads = [
        pltpu.make_async_copy(source, target, local_sem.at[i])
        for i, (source, target) in enumerate((
            (s_hbm, raw.at[pl.ds(0, 4)]), (columns_hbm, columns.at[0]), (home_hbm, home),
            (z_hbm, z_keep.at[0]), (y_hbm, y_keep.at[0]),
        ))
    ]

    def on_side(c, run):
        if c in inside:
            pl.when(inside[c])(run)
        else:
            run()

    def remote(source, target, s_sem, r_sem, device):
        return pltpu.make_async_remote_copy(
            src_ref=source, dst_ref=target, send_sem=s_sem, recv_sem=r_sem, device_id=device, device_id_type=MESH
        )

    for load in loads:
        load.start()
    barrier = pltpu.get_barrier_semaphore()

    def signal(semaphore, device):
        pl.semaphore_signal(semaphore, inc=1, device_id=device, device_id_type=MESH)

    @pl.when(high)
    def _():
        signal(barrier, place[5])

    moves = [
        remote(columns_hbm, columns.at[1], move.at[0], move.at[1], place[5]),
        remote(s_hbm, raw.at[pl.ds(4, 4)], move.at[2], move.at[3], place[5]),
    ]

    @pl.when(low)
    def _():
        pl.semaphore_wait(barrier, 1)
        signal(pair_sem, place[5])
        moves[1].start()
        moves[0].start()

    for c in LINKS:
        @pl.when(inside[c])
        def _():
            x, y, _ = place[c]
            signal(barrier, (x, y, 1))

    zero = jnp.zeros((BLOCK, BLOCK), jnp.bfloat16)
    raw[8] = zero

    loads[0].wait()

    @pl.when(high)
    def _():
        pl.semaphore_wait(pair_sem, 1)
        remote(raw.at[pl.ds(0, 4)], raw.at[pl.ds(4, 4)], move.at[2], move.at[3], place[5]).start()
        moves[0].start()
        pl.semaphore_wait(barrier, sum(jnp.where(inside[c], 2, 0) for c in LINKS))

    for load in loads[1:]:
        load.wait()

    def z_copy(c, end):
        return remote(z_hbm, z_keep.at[end], z_send.at[c - 1], z_recv.at[end - 1], place[c])

    y_copy = remote(y_hbm, y_keep.at[1], y_sem.at[0], y_sem.at[1], place[5])
    y_copy.start()
    z_copy(5, 5).start()
    moves[0].wait_recv()
    stay = home[0, 0] == gz
    base = jnp.where(stay, 0, 4)
    column = [jnp.where(stay, columns[0, 0, k], columns[1, 0, k]) for k in range(4)]
    other_column = [jnp.where(stay, columns[1, 0, k], columns[0, 0, k]) for k in range(4)]

    def pick(entries, wanted, first):
        index = jnp.int32(8)
        for k in (1, 2, 3):
            index = jnp.where(entries[k] == wanted, first + k, index)
        return index

    found, kept_found, keep_y, keep_z = {}, {}, {}, {}
    for c in SIDES:
        valid = inside.get(c, True)
        index = pick(column, slot[c], base)
        keep_y[c] = jnp.logical_and(y_keep[0, 0, slot[c]] == 1, valid)
        keep_z[c] = jnp.logical_and(z_keep[0, 0, slot[c]] == 1, valid)
        found[c] = jnp.where(valid, index, 8)
        kept_found[c] = jnp.where(keep_y[c], index, 8)

    moves[1].wait_recv()
    square = {0: raw[base]}
    own_out[...] = square[0]
    for c in LINKS:
        face_out[c] = raw[kept_found[c]]

    def send_faces(core):
        for c in LINKS:
            copy = remote(
                face_out.at[c], face_in.at[FACING[c]], send.at[c - 1], face_recv.at[FACING[c] - 1], place[c]
            )
            pl.when(jnp.logical_and(inside[c], core))(copy.start)

    def send_owns(core):
        for c in LINKS:
            copy = remote(
                own_out, own_in.at[FACING[c]], send.at[c - 1], own_recv.at[FACING[c] - 1], place[c]
            )
            pl.when(jnp.logical_and(inside[c], core))(copy.start)

    send_faces(high)
    send_owns(high)

    @pl.when(high)
    def _():
        signal(pair_sem, place[5])

    moves[0].wait_send()

    for c in LINKS:
        @pl.when(jnp.logical_not(inside[c]))
        def _():
            for buffer in (face_in, own_in, next_in, middle_in):
                buffer[c] = zero
            for i in range(7):
                z_keep[c, 0, i] = 0

    def send_to(source, target, sems):
        for c in SIDES:
            on_side(c, remote(source, target.at[FACING[c]], send.at[c - 1], sems.at[FACING[c] - 1], place[c]).start)

    def arrived(buffer, sems, c):
        on_side(c, remote(buffer.at[c], buffer.at[c], send.at[c - 1], sems.at[c - 1], place[c]).wait_recv)

    row = lax.broadcasted_iota(jnp.int32, (BLOCK, BLOCK), 0)
    lane = lax.broadcasted_iota(jnp.int32, (BLOCK, BLOCK), 1)
    lifted = jnp.where(row == lane, 1.5, 0.0).astype(jnp.float32)

    def half(x):
        return (x.astype(jnp.float32) * -0.5).astype(jnp.bfloat16)

    def centre(x):
        return (lifted - 0.5 * x.astype(jnp.float32)).astype(jnp.bfloat16)

    def kept(mask, x):
        return jnp.where(mask, x, jnp.zeros_like(x))


    middle = {0: centre(square[0])}
    inverse = {0: middle[0]}
    for c in SIDES:
        square[c] = raw[found[c]]
        middle[c] = half(raw[kept_found[c]])
        inverse[c] = kept(keep_z[c], middle[c])
    first = {c: dot(square[0], middle[c]) for c in (0,) + SIDES}
    moves[1].wait_send()

    @pl.when(low)
    def _():
        pl.semaphore_wait(pair_sem, 1)

    send_faces(low)
    send_owns(low)
    for c in LINKS:
        on_side(c, z_copy(c, FACING[c]).start)
    y_copy.wait_recv()
    near_index = pick(other_column, facing_slot[5], 4 - base)

    for c in LINKS:
        arrived(face_in, face_recv, c)
    near_face = {c: face_in[c] for c in LINKS}
    near_face[5] = raw[jnp.where(y_keep[1, 0, facing_slot[5]] == 1, near_index, 8)]
    total = first[0] - 0.5 * at_once([square[c] for c in SIDES], [near_face[c] for c in SIDES])
    square_next = {0: total.astype(jnp.bfloat16)}
    next_out[...] = square_next[0]
    send_to(next_out, next_in, next_recv)

    spread = dot(below([near_face[c] for c in SIDES]), middle[0])
    near_own, near_next = {5: raw[4 - base]}, {}
    for c in LINKS:
        arrived(own_in, own_recv, c)
    for i, c in enumerate(SIDES):
        if c in LINKS:
            near_own[c] = own_in[c]
        part = spread[i * BLOCK:(i + 1) * BLOCK]
        near_next[c] = (part - 0.5 * dot(near_own[c], near_face[c])).astype(jnp.bfloat16)
    quad = each([inverse[c] for c in (0,) + SIDES], [square_next[0]] + [near_next[c] for c in SIDES])
    last = {0: (lifted - 0.5 * quad).astype(jnp.bfloat16)}
    middle_out[...] = last[0]
    send_to(middle_out, middle_in, middle_recv)
    y_copy.wait_send()

    near_flag = {}
    for c in SIDES:
        on_side(c, z_copy(c, c).wait_recv)
        near_flag[c] = jnp.logical_and(z_keep[c, 0, facing_slot[c]] == 1, inside.get(c, True))
    near_centre, near_inverse, near_last, part_quad, part_z = {}, {}, {}, {}, {0: dot(last[0], inverse[0])}
    for c in SIDES:
        near_centre[c] = centre(near_own[c])
        square_next[c] = kept(keep_y[c], first[c] + dot(square[c], near_centre[c])).astype(jnp.bfloat16)
        part_quad[c] = dot(inverse[0], square_next[c])
        part_z[c] = dot(last[0], inverse[c])
        near_inverse[c] = kept(near_flag[c], half(near_face[c]))
        near_quad = dot(beside([near_inverse[c], near_centre[c]]), below([square_next[0], near_next[c]]))
        near_last[c] = (-0.5 * near_quad).astype(jnp.bfloat16)
    y_total = at_once([square_next[c] for c in (0,) + SIDES], [last[0]] + [near_last[c] for c in SIDES])
    y_out[0] = y_total.astype(jnp.bfloat16)
    z_out[facing_slot[5]] = zero
    y_out[facing_slot[5]] = zero

    for c in SIDES:
        arrived(next_in, next_recv, c)
    for c in SIDES:
        last[c] = kept(keep_y[c], -0.5 * (part_quad[c] + dot(inverse[c], next_in[c]))).astype(jnp.bfloat16)
    z_total, y_part = part_z[0], {}
    for c in SIDES:
        wide = dot(last[c], beside([near_inverse[c], near_centre[c]]))
        z_total = z_total + wide[:, :BLOCK]
        z_out[slot[c]] = kept(keep_z[c], part_z[c] + wide[:, BLOCK:]).astype(jnp.bfloat16)
    y_wide = dot(square_next[0], beside([last[c] for c in SIDES]))
    y_part = {c: y_wide[:, i * BLOCK:(i + 1) * BLOCK] for i, c in enumerate(SIDES)}
    z_out[0] = z_total.astype(jnp.bfloat16)

    for c in SIDES:
        arrived(middle_in, middle_recv, c)
    for c in SIDES:
        y_out[slot[c]] = kept(keep_y[c], y_part[c] + dot(square_next[c], middle_in[c])).astype(jnp.bfloat16)

    for c in SIDES:
        @functools.partial(on_side, c)
        def _():
            part = raw.at[pl.ds(0, 2 if c == 5 else 4)]
            remote(part, part, send.at[c - 1], face_recv.at[0], place[c]).wait_send()
            z_copy(c, c).wait_send()


def store(z_in, y_in, z_out, y_out, sem):
    copies = [pltpu.make_async_copy(z_in, z_out, sem.at[0]), pltpu.make_async_copy(y_in, y_out, sem.at[1])]
    for copy in copies:
        copy.start()
    for copy in copies:
        copy.wait()


def solution(mesh):
    sizes = (mesh.shape["gx"], mesh.shape["gy"])

    def step(s_blocks, s_columns, new_home, z_pattern, y_pattern):
        any_spec = pl.BlockSpec(memory_space=pl.ANY)
        vmem = pl.BlockSpec(memory_space=pltpu.VMEM)
        buffer = pltpu.VMEM((6, BLOCK, BLOCK), jnp.bfloat16)
        single = pltpu.VMEM((BLOCK, BLOCK), jnp.bfloat16)
        dma = pltpu.SemaphoreType.DMA
        z, y = pl.pallas_call(
            lambda *refs: kernel(sizes, *refs),
            name="newton_schulz",
            out_shape=(pltpu.VMEM((7, BLOCK, BLOCK), jnp.bfloat16),) * 2,
            in_specs=[any_spec] * 5,
            out_specs=(vmem, vmem),
            scratch_shapes=[
                pltpu.VMEM((9, BLOCK, BLOCK), jnp.bfloat16),
                pltpu.SMEM((2, 1, 4), jnp.int32),
                pltpu.SMEM((1, 1), jnp.int32),
                pltpu.SMEM((6, 1, 7), jnp.int32),
                pltpu.SMEM((2, 1, 7), jnp.int32),
                buffer, single, single, single,
                buffer, buffer, buffer, buffer,
                dma((5,)), pltpu.SemaphoreType.REGULAR, dma((4,)), dma((5,)), dma((5,)), dma((2,)),
                dma((5,)), dma((4,)), dma((4,)), dma((5,)), dma((5,)),
            ],
            compiler_params=pltpu.CompilerParams(collective_id=0, has_side_effects=True),
        )(s_blocks[0], s_columns, new_home.reshape(1, 1), z_pattern, y_pattern)
        z, y = pl.pallas_call(
            store,
            name="store",
            out_shape=(jax.ShapeDtypeStruct((7, BLOCK, BLOCK), jnp.bfloat16),) * 2,
            in_specs=[any_spec] * 2,
            out_specs=(any_spec,) * 2,
            scratch_shapes=[dma((2,))],
            compiler_params=pltpu.CompilerParams(vmem_limit_bytes=1 << 20),
        )(z, y)
        return jnp.transpose(z, (1, 0, 2))[None], jnp.transpose(y, (1, 0, 2))[None]

    row = P(("gx", "gy", "gz"))
    wide = P(("gx", "gy", "gz"), None)
    block = P(("gx", "gy", "gz"), None, None, None)
    return jax.shard_map(
        step, mesh=mesh, in_specs=(block, wide, row, wide, wide), out_specs=(block, block), check_vma=False
    )
```

```python
import functools

import jax
import jax.numpy as jnp
from jax import lax
from jax.experimental import pallas as pl
from jax.experimental.pallas import tpu as pltpu
from jax.sharding import PartitionSpec as P

MESH = pl.DeviceIdType.MESH
BLOCK = 128
LINKS = (1, 2, 3, 4)
SIDES = LINKS + (5,)
FACING = {1: 2, 2: 1, 3: 4, 4: 3, 5: 5}


def dot(a, b):
    return jnp.dot(a, b, preferred_element_type=jnp.float32)


def beside(parts):
    return jnp.concatenate(parts, axis=1)


def below(parts):
    return jnp.concatenate(parts, axis=0)


def at_once(lefts, rights):
    return dot(beside(lefts), below(rights))


def each(lefts, rights):
    return functools.reduce(jnp.add, [dot(left, right) for left, right in zip(lefts, rights)])


def kernel(
    sizes, s_hbm, columns_hbm, home_hbm, z_hbm, y_hbm, z_out, y_out,
    raw, columns, home, z_keep, y_keep, face_out, own_out, next_out, middle_out,
    face_in, own_in, next_in, middle_in, local_sem, pair_sem, move, z_send, z_recv, y_sem,
    send, face_recv, own_recv, next_recv, middle_recv,
):
    n_x, n_y = sizes
    gx, gy, gz = lax.axis_index("gx"), lax.axis_index("gy"), lax.axis_index("gz")
    place = {1: (gx - 1, gy, gz), 2: (gx + 1, gy, gz), 3: (gx, gy - 1, gz), 4: (gx, gy + 1, gz), 5: (gx, gy, 1 - gz)}
    inside = {1: gx > 0, 2: gx < n_x - 1, 3: gy > 0, 4: gy < n_y - 1}
    slot = {1: 1, 2: 2, 3: 3, 4: 4, 5: 6 - gz}
    facing_slot = {1: 2, 2: 1, 3: 4, 4: 3, 5: 5 + gz}
    low, high = gz == 0, gz == 1

    loads = [
        pltpu.make_async_copy(source, target, local_sem.at[i])
        for i, (source, target) in enumerate((
            (s_hbm, raw.at[pl.ds(0, 4)]), (columns_hbm, columns.at[0]), (home_hbm, home),
            (z_hbm, z_keep.at[0]), (y_hbm, y_keep.at[0]),
        ))
    ]

    def on_side(c, run):
        if c in inside:
            pl.when(inside[c])(run)
        else:
            run()

    def remote(source, target, s_sem, r_sem, device):
        return pltpu.make_async_remote_copy(
            src_ref=source, dst_ref=target, send_sem=s_sem, recv_sem=r_sem, device_id=device, device_id_type=MESH
        )

    for load in loads:
        load.start()
    barrier = pltpu.get_barrier_semaphore()

    def signal(semaphore, device):
        pl.semaphore_signal(semaphore, inc=1, device_id=device, device_id_type=MESH)

    @pl.when(high)
    def _():
        signal(barrier, place[5])

    moves = [
        remote(columns_hbm, columns.at[1], move.at[0], move.at[1], place[5]),
        remote(s_hbm, raw.at[pl.ds(4, 4)], move.at[2], move.at[3], place[5]),
    ]

    @pl.when(low)
    def _():
        pl.semaphore_wait(barrier, 1)
        signal(pair_sem, place[5])
        moves[0].start()
        moves[1].start()

    for c in LINKS:
        @pl.when(inside[c])
        def _():
            x, y, _ = place[c]
            signal(barrier, (x, y, 1))

    zero = jnp.zeros((BLOCK, BLOCK), jnp.bfloat16)
    raw[8] = zero

    loads[0].wait()

    @pl.when(high)
    def _():
        pl.semaphore_wait(pair_sem, 1)
        remote(raw.at[pl.ds(0, 4)], raw.at[pl.ds(4, 4)], move.at[2], move.at[3], place[5]).start()
        moves[0].start()
        pl.semaphore_wait(barrier, sum(jnp.where(inside[c], 2, 0) for c in LINKS))

    for load in loads[1:]:
        load.wait()

    def z_copy(c, end):
        return remote(z_hbm, z_keep.at[end], z_send.at[c - 1], z_recv.at[end - 1], place[c])

    y_copy = remote(y_hbm, y_keep.at[1], y_sem.at[0], y_sem.at[1], place[5])
    y_copy.start()
    z_copy(5, 5).start()
    moves[0].wait_recv()
    stay = home[0, 0] == gz
    base = jnp.where(stay, 0, 4)
    column = [jnp.where(stay, columns[0, 0, k], columns[1, 0, k]) for k in range(4)]
    other_column = [jnp.where(stay, columns[1, 0, k], columns[0, 0, k]) for k in range(4)]

    def pick(entries, wanted, first):
        index = jnp.int32(8)
        for k in (1, 2, 3):
            index = jnp.where(entries[k] == wanted, first + k, index)
        return index

    found, kept_found, keep_y, keep_z = {}, {}, {}, {}
    for c in SIDES:
        valid = inside.get(c, True)
        index = pick(column, slot[c], base)
        keep_y[c] = jnp.logical_and(y_keep[0, 0, slot[c]] == 1, valid)
        keep_z[c] = jnp.logical_and(z_keep[0, 0, slot[c]] == 1, valid)
        found[c] = jnp.where(valid, index, 8)
        kept_found[c] = jnp.where(keep_y[c], index, 8)

    moves[1].wait_recv()
    square = {0: raw[base]}
    own_out[...] = square[0]
    for c in LINKS:
        face_out[c] = raw[kept_found[c]]

    def send_faces(core):
        for c in LINKS:
            copy = remote(
                face_out.at[c], face_in.at[FACING[c]], send.at[c - 1], face_recv.at[FACING[c] - 1], place[c]
            )
            pl.when(jnp.logical_and(inside[c], core))(copy.start)

    def send_owns(core):
        for c in LINKS:
            copy = remote(
                own_out, own_in.at[FACING[c]], send.at[c - 1], own_recv.at[FACING[c] - 1], place[c]
            )
            pl.when(jnp.logical_and(inside[c], core))(copy.start)

    send_faces(high)
    send_owns(high)

    @pl.when(high)
    def _():
        signal(pair_sem, place[5])

    moves[0].wait_send()

    for c in LINKS:
        @pl.when(jnp.logical_not(inside[c]))
        def _():
            for buffer in (face_in, own_in, next_in, middle_in):
                buffer[c] = zero
            for i in range(7):
                z_keep[c, 0, i] = 0

    def send_to(source, target, sems):
        for c in (5,) + LINKS:
            on_side(c, remote(source, target.at[FACING[c]], send.at[c - 1], sems.at[FACING[c] - 1], place[c]).start)

    def arrived(buffer, sems, c):
        on_side(c, remote(buffer.at[c], buffer.at[c], send.at[c - 1], sems.at[c - 1], place[c]).wait_recv)

    row = lax.broadcasted_iota(jnp.int32, (BLOCK, BLOCK), 0)
    lane = lax.broadcasted_iota(jnp.int32, (BLOCK, BLOCK), 1)
    lifted = jnp.where(row == lane, 1.5, 0.0).astype(jnp.float32)

    def half(x):
        return (x.astype(jnp.float32) * -0.5).astype(jnp.bfloat16)

    def centre(x):
        return (lifted - 0.5 * x.astype(jnp.float32)).astype(jnp.bfloat16)

    def kept(mask, x):
        return jnp.where(mask, x, jnp.zeros_like(x))


    middle = {0: centre(square[0])}
    inverse = {0: middle[0]}
    for c in SIDES:
        square[c] = raw[found[c]]
        middle[c] = half(raw[kept_found[c]])
        inverse[c] = kept(keep_z[c], middle[c])
    first = {c: dot(square[0], middle[c]) for c in (0,) + SIDES}
    moves[1].wait_send()

    @pl.when(low)
    def _():
        pl.semaphore_wait(pair_sem, 1)

    send_faces(low)
    send_owns(low)
    for c in LINKS:
        on_side(c, z_copy(c, FACING[c]).start)
    y_copy.wait_recv()
    near_index = pick(other_column, facing_slot[5], 4 - base)

    for c in LINKS:
        arrived(face_in, face_recv, c)
    near_face = {c: face_in[c] for c in LINKS}
    near_face[5] = raw[jnp.where(y_keep[1, 0, facing_slot[5]] == 1, near_index, 8)]
    total = first[0] - 0.5 * at_once([square[c] for c in SIDES], [near_face[c] for c in SIDES])
    square_next = {0: total.astype(jnp.bfloat16)}
    next_out[...] = square_next[0]
    send_to(next_out, next_in, next_recv)

    spread = dot(below([near_face[c] for c in SIDES]), middle[0])
    near_own, near_next = {5: raw[4 - base]}, {}
    for c in LINKS:
        arrived(own_in, own_recv, c)
    for i, c in enumerate(SIDES):
        if c in LINKS:
            near_own[c] = own_in[c]
        part = spread[i * BLOCK:(i + 1) * BLOCK]
        near_next[c] = (part - 0.5 * dot(near_own[c], near_face[c])).astype(jnp.bfloat16)
    quad = each([inverse[c] for c in (0,) + SIDES], [square_next[0]] + [near_next[c] for c in SIDES])
    last = {0: (lifted - 0.5 * quad).astype(jnp.bfloat16)}
    middle_out[...] = last[0]
    send_to(middle_out, middle_in, middle_recv)
    y_copy.wait_send()

    near_flag = {}
    for c in SIDES:
        on_side(c, z_copy(c, c).wait_recv)
        near_flag[c] = jnp.logical_and(z_keep[c, 0, facing_slot[c]] == 1, inside.get(c, True))
    near_centre, near_inverse, near_last, part_quad, part_z = {}, {}, {}, {}, {0: dot(last[0], inverse[0])}
    for c in SIDES:
        near_centre[c] = centre(near_own[c])
        square_next[c] = kept(keep_y[c], first[c] + dot(square[c], near_centre[c])).astype(jnp.bfloat16)
        part_quad[c] = dot(inverse[0], square_next[c])
        part_z[c] = dot(last[0], inverse[c])
        near_inverse[c] = kept(near_flag[c], half(near_face[c]))
        near_quad = dot(beside([near_inverse[c], near_centre[c]]), below([square_next[0], near_next[c]]))
        near_last[c] = (-0.5 * near_quad).astype(jnp.bfloat16)
    y_total = at_once([square_next[c] for c in (0,) + SIDES], [last[0]] + [near_last[c] for c in SIDES])
    y_out[0] = y_total.astype(jnp.bfloat16)
    z_out[facing_slot[5]] = zero
    y_out[facing_slot[5]] = zero

    for c in SIDES:
        arrived(next_in, next_recv, c)
    for c in SIDES:
        last[c] = kept(keep_y[c], -0.5 * (part_quad[c] + dot(inverse[c], next_in[c]))).astype(jnp.bfloat16)
    z_total, y_part = part_z[0], {}
    for c in SIDES:
        wide = dot(last[c], beside([near_inverse[c], near_centre[c]]))
        z_total = z_total + wide[:, :BLOCK]
        z_out[slot[c]] = kept(keep_z[c], part_z[c] + wide[:, BLOCK:]).astype(jnp.bfloat16)
    y_wide = dot(square_next[0], beside([last[c] for c in SIDES]))
    y_part = {c: y_wide[:, i * BLOCK:(i + 1) * BLOCK] for i, c in enumerate(SIDES)}
    z_out[0] = z_total.astype(jnp.bfloat16)

    for c in SIDES:
        arrived(middle_in, middle_recv, c)
    for c in SIDES:
        y_out[slot[c]] = kept(keep_y[c], y_part[c] + dot(square_next[c], middle_in[c])).astype(jnp.bfloat16)

    for c in SIDES:
        @functools.partial(on_side, c)
        def _():
            part = raw.at[pl.ds(0, 2 if c == 5 else 4)]
            remote(part, part, send.at[c - 1], face_recv.at[0], place[c]).wait_send()
            z_copy(c, c).wait_send()


def store(z_in, y_in, z_out, y_out, sem):
    copies = [pltpu.make_async_copy(z_in, z_out, sem.at[0]), pltpu.make_async_copy(y_in, y_out, sem.at[1])]
    for copy in copies:
        copy.start()
    for copy in copies:
        copy.wait()


def solution(mesh):
    sizes = (mesh.shape["gx"], mesh.shape["gy"])

    def step(s_blocks, s_columns, new_home, z_pattern, y_pattern):
        any_spec = pl.BlockSpec(memory_space=pl.ANY)
        vmem = pl.BlockSpec(memory_space=pltpu.VMEM)
        buffer = pltpu.VMEM((6, BLOCK, BLOCK), jnp.bfloat16)
        single = pltpu.VMEM((BLOCK, BLOCK), jnp.bfloat16)
        dma = pltpu.SemaphoreType.DMA
        z, y = pl.pallas_call(
            lambda *refs: kernel(sizes, *refs),
            name="newton_schulz",
            out_shape=(pltpu.VMEM((7, BLOCK, BLOCK), jnp.bfloat16),) * 2,
            in_specs=[any_spec] * 5,
            out_specs=(vmem, vmem),
            scratch_shapes=[
                pltpu.VMEM((9, BLOCK, BLOCK), jnp.bfloat16),
                pltpu.SMEM((2, 1, 4), jnp.int32),
                pltpu.SMEM((1, 1), jnp.int32),
                pltpu.SMEM((6, 1, 7), jnp.int32),
                pltpu.SMEM((2, 1, 7), jnp.int32),
                buffer, single, single, single,
                buffer, buffer, buffer, buffer,
                dma((5,)), pltpu.SemaphoreType.REGULAR, dma((4,)), dma((5,)), dma((5,)), dma((2,)),
                dma((5,)), dma((4,)), dma((4,)), dma((5,)), dma((5,)),
            ],
            compiler_params=pltpu.CompilerParams(collective_id=0, has_side_effects=True),
        )(s_blocks[0], s_columns, new_home.reshape(1, 1), z_pattern, y_pattern)
        z, y = pl.pallas_call(
            store,
            name="store",
            out_shape=(jax.ShapeDtypeStruct((7, BLOCK, BLOCK), jnp.bfloat16),) * 2,
            in_specs=[any_spec] * 2,
            out_specs=(any_spec,) * 2,
            scratch_shapes=[dma((2,))],
            compiler_params=pltpu.CompilerParams(vmem_limit_bytes=1 << 20),
        )(z, y)
        return jnp.transpose(z, (1, 0, 2))[None], jnp.transpose(y, (1, 0, 2))[None]

    row = P(("gx", "gy", "gz"))
    wide = P(("gx", "gy", "gz"), None)
    block = P(("gx", "gy", "gz"), None, None, None)
    return jax.shard_map(
        step, mesh=mesh, in_specs=(block, wide, row, wide, wide), out_specs=(block, block), check_vma=False
    )
```
